128 devices in a mesh: section: 4 (over z), tile: 32 (over x, y, core).
Axes of the slice: x: 4, y: 4, z: 4, core: 2. Of those that a mesh axis runs over, the one named last changes fastest.
Arguments:
- surface: float32 [4, 4096, 16, 128], P('section', 'tile'), may hold values from -6 to 6
- surface_mask: int32 [4, 4096, 128], P('section', 'tile'), may hold values 0 or 1
- kappa: float32 [4, 16], P('section'), may hold values from 4 to 32
- remap_weights: bfloat16 [4, 4096, 4, 128, 128], P('section', 'tile'), may hold values from -0.25 to 0.25
- remap_columns: int32 [4, 4096, 4], P('section', 'tile'), may hold values from 0 to 16383, as said below
Outputs:
- new_surface: float32 [4, 4096, 16, 128], P('section', 'tile')
The draws below stay inside these ranges and needn't reach their ends.
Inputs may be any that keep to these rules, and one draw needn't show every extreme that they name: `remap_columns`: for section 0 (atmosphere) every source block lies in sections 1 to 3; for sections 1 to 3 it lies in section 0. The source row lies in the destination row's tile of 128 rows or in one of the two tiles beside it.
All inputs are finite; a program needn't handle non-finite values. No bound on the sum of `surface_mask` on one device may be relied on, other than what follows from the above.
Results may differ from the reference program's by a relative error of at most 0.0011.
Values may be sent and summed in bfloat16 or wider, within the bound.
A program may use at most 128 MiB of HBM per device.

```python
import math
import jax
import jax.numpy as jnp
from jax import lax

FIELDS = 16
BLOCK = 128
BLOCKS = 4
ROWS_DEV = 128
SWEEPS = 4
ROWS = 4096
N_SECTION = 4
N_TILE = 32


def draw_remap_columns(key, part):
    first_key, second_key, third_key = jax.random.split(jax.random.fold_in(key, 71), 3)
    array_shape = (N_SECTION, ROWS, BLOCKS)
    dest_row = jnp.arange(ROWS, dtype=jnp.int32)[None, :, None]
    dest_tile = dest_row // ROWS_DEV
    tile_step = jax.random.randint(first_key, array_shape, -1, 2, dtype=jnp.int32)
    source_tile = jnp.clip(dest_tile + tile_step, 0, N_TILE - 1)
    row_offset = jax.random.randint(second_key, array_shape, 0, ROWS_DEV, dtype=jnp.int32)
    other_section = jax.random.randint(third_key, array_shape, 1, N_SECTION, dtype=jnp.int32)
    section_ids = jnp.arange(N_SECTION, dtype=jnp.int32)[:, None, None]
    source_section = jnp.where(section_ids == 0, other_section, 0)
    columns = source_section * ROWS + source_tile * ROWS_DEV + row_offset
    columns = columns.at[0, ROWS - 1, 0].set(N_SECTION * ROWS - 1)
    columns = columns.at[1, 0, 0].set(0)
    return columns.astype(jnp.int32)


def with_ends(values, rng, low, high):
    shape = values.shape
    place = [jax.random.randint(jax.random.fold_in(rng, axis), (), 0, shape[axis]) for axis in range(len(shape))]
    values = values.at[tuple(place)].set(low)
    longest = shape.index(max(shape))
    place[longest] = (place[longest] + 1) % shape[longest]
    return values.at[tuple(place)].set(high)


def block_scale(stream_key, dims, cuts, low, top_value):
    loudness, own = 1.0, jax.random.fold_in(stream_key, 6)
    for axis_at, parts in cuts:
        steps = jnp.exp(jax.random.uniform(jax.random.fold_in(own, axis_at), (parts,), jnp.float32, low / len(cuts), top_value / len(cuts)))
        loudness = loudness * jnp.repeat(steps, dims[axis_at] // parts).reshape([-1 if axis == axis_at else 1 for axis in range(len(dims))])
    return loudness


def centred(rng, shape, scale, limit, cuts=(), held_as=jnp.bfloat16):
    factor_of = block_scale(rng, shape, cuts, -0.22, 0.18) if cuts else 1.0
    array = jax.random.normal(rng, shape, jnp.float32) * scale * factor_of
    return jnp.minimum(jnp.maximum(array, -limit), limit).astype(held_as)


def setup_inputs(seed: int = 0) -> dict:
    seeds = jax.random.split(jax.random.key(seed), 6)
    surface = centred(seeds[0], (N_SECTION, ROWS, FIELDS, BLOCK), 1.0, 6.0, ((0, 4), (1, 32)), jnp.float32)
    surface_mask = with_ends((jax.random.randint(seeds[1], (N_SECTION, ROWS, BLOCK), 0, 4) < 3).astype(jnp.int32), jax.random.fold_in(seeds[1], 1), 0, 1)
    kappa = jnp.clip(jnp.exp(math.log(32.0) - 2.0794415 * jax.random.uniform(seeds[2], (N_SECTION, FIELDS), jnp.float32) ** block_scale(seeds[2], (N_SECTION, FIELDS), ((0, 4),), -0.2, 0.2)), 4.0, 32.0)
    remap_weights = centred(seeds[3], (N_SECTION, ROWS, BLOCKS, BLOCK, BLOCK), (BLOCKS * BLOCK) ** -0.5, 0.25, ((0, 4), (1, 32)))
    remap_columns = draw_remap_columns(jax.random.fold_in(seeds[5], 71), 0)
    return {"surface": surface, "surface_mask": surface_mask, "kappa": kappa, "remap_weights": remap_weights, "remap_columns": remap_columns}


time_step = 0.5
zonal_ratio = 0.25


def relaxation(right_side, kappa_row):
    meridional = kappa_row[None, :, None]
    zonal_coef = zonal_ratio * meridional
    denominator = 1.0 + 2.0 * meridional + 2.0 * zonal_coef
    iterate = right_side
    for sweep_index in range(SWEEPS):
        padded = jnp.pad(iterate, ((1, 1), (0, 0), (0, 0)))
        vertical = padded[:-2] + padded[2:]
        zonal_sum = jnp.roll(iterate, 1, 2) + jnp.roll(iterate, -1, 2)
        iterate = (right_side + meridional * vertical + zonal_coef * zonal_sum) / denominator
    return iterate


def remap_section(sent_blocks, weights, columns):
    def one_tile(pieces):
        tile_weights, tile_columns = pieces
        picked = jnp.take(sent_blocks, tile_columns.reshape(-1), axis=0)
        picked = picked.reshape((ROWS_DEV, BLOCKS) + sent_blocks.shape[1:])
        return jnp.einsum("rkij,rkfj->rfi", tile_weights.astype(jnp.float32), picked.astype(jnp.float32), precision=lax.Precision.HIGHEST)

    weight_groups = weights.reshape((N_TILE, ROWS_DEV) + weights.shape[1:])
    column_groups = columns.reshape(N_TILE, ROWS_DEV, BLOCKS)
    result = lax.map(one_tile, (weight_groups, column_groups))
    return result.reshape((ROWS,) + result.shape[2:])


def reference(surface, surface_mask, kappa, remap_weights, remap_columns):
    sent = surface.astype(jnp.bfloat16)
    sent_blocks = sent.reshape((N_SECTION * ROWS,) + sent.shape[2:])
    outputs = []
    for section_index in range(N_SECTION):
        forcing = remap_section(sent_blocks, remap_weights[section_index], remap_columns[section_index])
        mask_values = surface_mask[section_index].astype(jnp.float32)[:, None, :]
        right_side = surface[section_index] + time_step * mask_values * forcing
        outputs.append(relaxation(right_side, kappa[section_index]))
    return jnp.stack(outputs, axis=0)
```

```python
import functools

import jax
import jax.numpy as jnp
from jax import lax
from jax.experimental import pallas as pl
from jax.experimental.pallas import tpu as pltpu
from jax.sharding import PartitionSpec as P

SWEEPS = 4
TIME_STEP = 0.5
ZONAL_RATIO = 0.25

CHUNK = 16
GROUP = 28
WPIECES = 16

NT = (((1,), (1,)), ((), ()))
F32 = jnp.float32


def remote(src, dst, send_sem, recv_sem, where):
    return pltpu.make_async_remote_copy(
        src_ref=src, dst_ref=dst, send_sem=send_sem, recv_sem=recv_sem,
        device_id=where, device_id_type=pl.DeviceIdType.MESH,
    )


def kernel(
    tiles, surf_hbm, mask_hbm, kappa_hbm, w_hbm, cols_hbm, out,
    surf, mask, kappa, w, cols, sent, win, relay, edge, near, halo,
    surf_sem, w_sem, in_sem,
    z_send, z_recv, up_send, down_send, low_recv, high_recv, relay_recv, halo_send, halo_recv,
):
    rows, fields, cells = surf.shape
    blocks = w.shape[1]
    chunks = rows // CHUNK
    half = chunks // 2
    total = rows * tiles
    s = lax.axis_index("section")
    t = lax.axis_index("tile")
    s_up, s_down = lax.rem(s + 1, 4), lax.rem(s + 3, 4)
    has_low, has_high = t > 0, t < tiles - 1

    surf_in = [
        pltpu.make_async_copy(
            surf_hbm.at[0, pl.ds(p * (rows // 4), rows // 4)], surf.at[pl.ds(p * (rows // 4), rows // 4)], surf_sem.at[p]
        )
        for p in range(4)
    ]
    for copy in surf_in:
        copy.start()
    small_in = [
        pltpu.make_async_copy(cols_hbm, cols, in_sem.at[0]),
        pltpu.make_async_copy(mask_hbm.at[0], mask, in_sem.at[1]),
        pltpu.make_async_copy(kappa_hbm, kappa, in_sem.at[2]),
    ]
    for copy in small_in:
        copy.start()
    piece = rows // WPIECES
    w_in = [
        pltpu.make_async_copy(w_hbm.at[0, pl.ds(p * piece, piece)], w.at[pl.ds(p * piece, piece)], w_sem.at[p])
        for p in range(WPIECES)
    ]
    for copy in w_in:
        copy.start()

    barrier = pltpu.get_barrier_semaphore()
    for where in ({"section": s_up}, {"section": s_down}):
        pl.semaphore_signal(barrier, inc=1, device_id=where, device_id_type=pl.DeviceIdType.MESH)

    @pl.when(has_low)
    def _():
        pl.semaphore_signal(barrier, inc=1, device_id={"tile": t - 1}, device_id_type=pl.DeviceIdType.MESH)

    @pl.when(has_high)
    def _():
        pl.semaphore_signal(barrier, inc=1, device_id={"tile": t + 1}, device_id_type=pl.DeviceIdType.MESH)

    for p in range(4):
        surf_in[p].wait()
        part = pl.ds(p * (rows // 4), rows // 4)
        sent[part] = surf[part].astype(jnp.bfloat16)

    pl.semaphore_wait(barrier, 2 + has_low.astype(jnp.int32) + has_high.astype(jnp.int32))

    def at(start, q):
        return win.at[pl.ds(start + q * CHUNK, CHUNK)]

    def mine(q):
        return sent.at[pl.ds(q * CHUNK, CHUNK)]

    def to_low(base, q, n):
        return remote(at(base + rows, q), at(base + 2 * rows, q), down_send.at[n], high_recv.at[n], {"tile": t - 1})

    def to_high(base, q, n):
        return remote(at(base + rows, q), at(base, q), up_send.at[n], low_recv.at[n], {"tile": t + 1})

    def spread(base, q, n):
        @pl.when(has_low)
        def _():
            to_low(base, q, n).start()

        @pl.when(has_high)
        def _():
            to_high(base, q, n).start()

    def arrived(base, q, n):
        remote(mine(q), at(base + rows, q), z_send.at[n], z_recv.at[n], {"section": s_up}).wait_recv()

    def finish(count):
        def step(n, _):
            base, q = (n // chunks) * (3 * rows), lax.rem(n, chunks)

            @pl.when(has_low)
            def _():
                to_high(base, q, n).wait_recv()

            @pl.when(has_high)
            def _():
                to_low(base, q, n).wait_recv()

            return 0

        lax.fori_loop(0, count, step, 0)

    def finish_sends(count):
        def step(n, _):
            base, q = (n // chunks) * (3 * rows), lax.rem(n, chunks)

            @pl.when(has_low)
            def _():
                to_low(base, q, n).wait_send()

            @pl.when(has_high)
            def _():
                to_high(base, q, n).wait_send()

            return 0

        lax.fori_loop(0, count, step, 0)

    @pl.when(s == 0)
    def _():
        for q in range(chunks):
            remote(mine(q), at(rows, q), z_send.at[q], z_recv.at[q], {"section": s_up}).start()
            other = (q + half) % chunks
            remote(mine(other), at(rows, other), z_send.at[chunks + other], z_recv.at[other], {"section": s_down}).start()

        def direct(q, _):
            for src in (0, 2):
                n = src * chunks + q
                arrived(src * 3 * rows, q, n)
                spread(src * 3 * rows, q, n)
            return 0

        lax.fori_loop(0, chunks, direct, 0)

        def relayed(q, _):
            for h in range(2):
                n = chunks + h * half + q
                arrived(3 * rows, h * half + q, n)
                spread(3 * rows, h * half + q, n)
            return 0

        lax.fori_loop(0, half, relayed, 0)
        finish(3 * chunks)

    @pl.when((s == 1) | (s == 3))
    def _():
        h = s // 2
        base = (s - 1) * (3 * rows)
        far = 2
        for q in range(chunks):
            remote(mine(q), at(base + rows, q), z_send.at[q], z_recv.at[(s - 1) * chunks + q], {"section": 0}).start()

        def step(q, _):
            own = h * half + q
            held = relay.at[pl.ds(q * CHUNK, CHUNK)]
            arrived(0, own, own)
            remote(at(rows, own), at(rows, own), z_send.at[chunks + half + q], z_recv.at[own], {"section": far}).start()
            spread(0, own, own)
            remote(mine(q), held, z_send.at[q], relay_recv.at[q], {"section": far}).wait_recv()
            remote(
                held, at(4 * rows, own), z_send.at[chunks + q], z_recv.at[chunks + own], {"section": 0}
            ).start()
            return 0

        lax.fori_loop(0, half, step, 0)

        def rest(q, _):
            other = (1 - h) * half + q
            arrived(0, other, other)
            spread(0, other, other)
            return 0

        lax.fori_loop(0, half, rest, 0)
        finish(chunks)

    @pl.when(s == 2)
    def _():
        for q in range(half):
            held = relay.at[pl.ds(q * CHUNK, CHUNK)]
            remote(mine(q), held, z_send.at[q], relay_recv.at[q], {"section": 1}).start()
            remote(mine(half + q), held, z_send.at[half + q], relay_recv.at[q], {"section": 3}).start()

        def step(q, _):
            for n in (q, half + q):
                arrived(0, n, n)
                spread(0, n, n)
            return 0

        lax.fori_loop(0, half, step, 0)
        finish(chunks)

    for copy in small_in:
        copy.wait()
    for copy in w_in:
        copy.wait()

    offset = (1 - t) * rows - jnp.where(s == 0, 3 * rows, 0)
    lane = lax.broadcasted_iota(jnp.int32, (fields, fields), 1)
    sub = lax.broadcasted_iota(jnp.int32, (fields, fields), 0)
    diag = jnp.where(lane == sub, jnp.broadcast_to(kappa[0:1, :], (fields, fields)), 0.0)
    kap = jnp.broadcast_to(jnp.sum(diag, axis=1, keepdims=True), (fields, cells))
    inv = 1.0 / (1.0 + 2.0 * kap + 2.0 * (ZONAL_RATIO * kap))
    a = kap * inv
    b = ZONAL_RATIO * kap * inv

    def forced(r):
        picks, weights = [], []
        for k in range(blocks):
            c = cols[k, r]
            place = c - (c // total) * (total - 3 * rows) + offset
            picks.append(win[jnp.clip(place, 0, 9 * rows - 1)])
            weights.append(w[r, k])
        forcing = lax.dot_general(
            jnp.concatenate(picks, axis=1), jnp.concatenate(weights, axis=1), NT, preferred_element_type=F32
        )
        scale = TIME_STEP * mask[pl.ds(r, 1), :].astype(F32)
        return surf[r] + scale * forcing

    def swept(base, low, mid, high):
        zonal = pltpu.roll(mid, 1, 1) + pltpu.roll(mid, cells - 1, 1)
        return base + a * (low + high) + b * zonal

    def advance(state, row):
        levels, bases = state
        levels, bases = [list(x) for x in levels], list(bases)
        bases.append(row * inv)
        levels[0].append(row)
        new = None
        for n in range(SWEEPS):
            if len(levels[n]) < 3:
                return (levels, bases), None
            new = swept(bases[-2 - n], *levels[n][-3:])
            levels[n] = levels[n][-2:]
            if n + 1 < SWEEPS:
                levels[n + 1].append(new)
        return (levels, bases[-SWEEPS - 1:]), new

    low_rows = [forced(r) for r in range(SWEEPS)]
    high_rows = [forced(rows - SWEEPS + r) for r in range(SWEEPS)]
    for r in range(SWEEPS):
        edge[0, r] = low_rows[r]
        edge[1, r] = high_rows[r]
    halo_low = remote(edge.at[0], halo.at[1], halo_send.at[0], halo_recv.at[1], {"tile": t - 1})
    halo_high = remote(edge.at[1], halo.at[0], halo_send.at[1], halo_recv.at[0], {"tile": t + 1})
    pl.when(has_low)(halo_low.start)
    pl.when(has_high)(halo_high.start)

    state = ([[] for _ in range(SWEEPS)], [])
    for r in range(2 * SWEEPS):
        if r < SWEEPS:
            row = low_rows[r]
        else:
            row = forced(r)
            near[0, r - SWEEPS] = row
        state, done = advance(state, row)
        if done is not None:
            out[0, r - SWEEPS] = done

    def pack(state):
        levels, bases = state
        return tuple(x for level in levels for x in level) + tuple(bases[-SWEEPS:])

    def unpack(flat):
        return [list(flat[2 * n : 2 * n + 2]) for n in range(SWEEPS)], list(flat[2 * SWEEPS :])

    first = 2 * SWEEPS
    count = (rows - 2 * SWEEPS - first) // GROUP

    def group(g, flat):
        state = unpack(flat)
        for u in range(GROUP):
            r = first + g * GROUP + u
            state, done = advance(state, forced(r))
            out[0, r - SWEEPS] = done
        return pack(state)

    state = unpack(lax.fori_loop(0, count, group, pack(state)))
    for r in range(first + count * GROUP, rows):
        if r < rows - SWEEPS:
            row = forced(r)
            if r >= rows - 2 * SWEEPS:
                near[1, r - (rows - 2 * SWEEPS)] = row
        else:
            row = edge[1, r - (rows - SWEEPS)]
        state, done = advance(state, row)
        out[0, r - SWEEPS] = done

    pl.when(has_low)(halo_high.wait_recv)
    pl.when(has_high)(halo_low.wait_recv)

    def end_rows(values, outside, lost):
        values = [jnp.where(lost, 0.0, v) if outside(i) else v for i, v in enumerate(values)]
        bases = [v * inv for v in values]
        level = values
        for n in range(SWEEPS):
            level = [
                jnp.where(lost, 0.0, v) if outside(n + 1 + i) else v
                for i, v in enumerate(
                    swept(bases[n + i], *level[i - 1 : i + 2]) for i in range(1, len(level) - 1)
                )
            ]
        return level

    low_values = [halo[0, r] for r in range(SWEEPS)] + [edge[0, r] for r in range(SWEEPS)]
    low_values += [near[0, r] for r in range(SWEEPS)]
    for r, v in enumerate(end_rows(low_values, lambda i: i < SWEEPS, jnp.logical_not(has_low))):
        out[0, r] = v
    high_values = [near[1, r] for r in range(SWEEPS)] + [edge[1, r] for r in range(SWEEPS)]
    high_values += [halo[1, r] for r in range(SWEEPS)]
    for r, v in enumerate(end_rows(high_values, lambda i: i >= 2 * SWEEPS, jnp.logical_not(has_high))):
        out[0, rows - SWEEPS + r] = v

    pl.when(has_low)(halo_low.wait_send)
    pl.when(has_high)(halo_high.wait_send)

    def sent_out(count):
        def step(n, _):
            remote(mine(0), at(rows, 0), z_send.at[n], z_recv.at[0], {"section": s_up}).wait_send()
            return 0

        lax.fori_loop(0, count, step, 0)

    sent_out(jnp.where(s == 2, chunks, 2 * chunks))
    finish_sends(jnp.where(s == 0, 3 * chunks, chunks))


def body(tiles, surface, surface_mask, kappa, remap_weights, remap_columns):
    rows, fields, cells = surface.shape[1:]
    blocks = remap_weights.shape[2]
    chunks = rows // CHUNK
    half = chunks // 2
    block = (rows, fields, cells)
    dma = pltpu.SemaphoreType.DMA
    bf16 = jnp.bfloat16
    return pl.pallas_call(
        functools.partial(kernel, tiles),
        out_shape=jax.ShapeDtypeStruct(surface.shape, F32),
        in_specs=[pl.BlockSpec(memory_space=pltpu.HBM)] * 5,
        out_specs=pl.BlockSpec(memory_space=pltpu.VMEM),
        scratch_shapes=[
            pltpu.VMEM(block, F32),
            pltpu.VMEM((rows, cells), jnp.int32),
            pltpu.VMEM((1, fields), F32),
            pltpu.VMEM((rows, blocks, cells, cells), bf16),
            pltpu.SMEM((blocks, rows), jnp.int32),
            pltpu.VMEM(block, bf16),
            pltpu.VMEM((9 * rows, fields, cells), bf16),
            pltpu.VMEM((rows // 2, fields, cells), bf16),
            pltpu.VMEM((2, SWEEPS, fields, cells), F32),
            pltpu.VMEM((2, SWEEPS, fields, cells), F32),
            pltpu.VMEM((2, SWEEPS, fields, cells), F32),
            dma((4,)),
            dma((WPIECES,)),
            dma((3,)),
            dma((2 * chunks,)),
            dma((3 * chunks,)),
            dma((3 * chunks,)),
            dma((3 * chunks,)),
            dma((3 * chunks,)),
            dma((3 * chunks,)),
            dma((half,)),
            dma((2,)),
            dma((2,)),
        ],
        compiler_params=pltpu.CompilerParams(
            collective_id=0, has_side_effects=True, vmem_limit_bytes=48 * 1024 * 1024
        ),
        name="remap_and_sweep",
    )(surface, surface_mask, kappa, remap_weights, remap_columns[0].T)


def solution(mesh):
    return jax.shard_map(
        functools.partial(body, mesh.shape["tile"]),
        mesh=mesh,
        in_specs=(
            P("section", "tile", None, None),
            P("section", "tile", None),
            P("section", None),
            P("section", "tile", None, None, None),
            P("section", "tile", None),
        ),
        out_specs=P("section", "tile", None, None),
        check_vma=False,
    )
```

```python
import functools

import jax
import jax.numpy as jnp
from jax import lax
from jax.experimental import pallas as pl
from jax.experimental.pallas import tpu as pltpu
from jax.sharding import PartitionSpec as P

SWEEPS = 4
TIME_STEP = 0.5
ZONAL_RATIO = 0.25

CHUNK = 16
GROUP = 28
WPIECES = 32

NN = (((1,), (0,)), ((), ()))
F32 = jnp.float32


def remote(src, dst, send_sem, recv_sem, where):
    return pltpu.make_async_remote_copy(
        src_ref=src, dst_ref=dst, send_sem=send_sem, recv_sem=recv_sem,
        device_id=where, device_id_type=pl.DeviceIdType.MESH,
    )


def kernel(
    tiles, surf_hbm, mask_hbm, kappa_hbm, w_hbm, cols_hbm, out_hbm,
    surf, mask, kappa, w, cols, place, index, sent, win, relay, edge, near, halo, out,
    surf_sem, w_sem, in_sem, out_sem,
    z_send, z_recv, up_send, down_send, low_recv, high_recv, relay_recv, halo_send, halo_recv,
):
    rows, fields, cells = surf.shape
    blocks = w.shape[1]
    chunks = rows // CHUNK
    half = chunks // 2
    total = rows * tiles
    s = lax.axis_index("section")
    t = lax.axis_index("tile")
    s_up, s_down = lax.rem(s + 1, 4), lax.rem(s + 3, 4)
    has_low, has_high = t > 0, t < tiles - 1

    barrier = pltpu.get_barrier_semaphore()
    for where in ({"section": s_up}, {"section": s_down}):
        pl.semaphore_signal(barrier, inc=1, device_id=where, device_id_type=pl.DeviceIdType.MESH)

    @pl.when(has_low)
    def _():
        pl.semaphore_signal(barrier, inc=1, device_id={"tile": t - 1}, device_id_type=pl.DeviceIdType.MESH)

    @pl.when(has_high)
    def _():
        pl.semaphore_signal(barrier, inc=1, device_id={"tile": t + 1}, device_id_type=pl.DeviceIdType.MESH)

    surf_in = [
        pltpu.make_async_copy(
            surf_hbm.at[0, pl.ds(p * (rows // 4), rows // 4)], surf.at[pl.ds(p * (rows // 4), rows // 4)], surf_sem.at[p]
        )
        for p in range(4)
    ]
    for copy in surf_in:
        copy.start()
    small_in = [
        pltpu.make_async_copy(cols_hbm, cols, in_sem.at[0]),
        pltpu.make_async_copy(mask_hbm.at[0], mask, in_sem.at[1]),
        pltpu.make_async_copy(kappa_hbm, kappa, in_sem.at[2]),
    ]
    for copy in small_in:
        copy.start()
    piece = rows // WPIECES

    def w_in(p):
        part = pl.ds(p * piece, piece)
        return pltpu.make_async_copy(w_hbm.at[0, part], w.at[part], w_sem.at[p])

    def turn(p, _):
        w_in(p).wait()
        for r in range(piece):
            for k in range(blocks):
                w[p * piece + r, k] = w[p * piece + r, k].T
        return 0

    for p in range(4):
        surf_in[p].wait()
        part = pl.ds(p * (rows // 4), rows // 4)
        sent[part] = surf[part].astype(jnp.bfloat16)
    for p in range(WPIECES):
        w_in(p).start()

    small_in[0].wait()
    offset = (1 - t) * rows - jnp.where(s == 0, 3 * rows, 0)
    column = cols[...]
    place[...] = jnp.clip(column - (column // total) * (total - 3 * rows) + offset, 0, 9 * rows - 1)
    place_out = pltpu.make_async_copy(place, index, in_sem.at[3])
    place_out.start()

    pl.semaphore_wait(barrier, 2 + has_low.astype(jnp.int32) + has_high.astype(jnp.int32))

    def at(start, q):
        return win.at[pl.ds(start + q * CHUNK, CHUNK)]

    def mine(q):
        return sent.at[pl.ds(q * CHUNK, CHUNK)]

    def to_low(base, q, n):
        return remote(at(base + rows, q), at(base + 2 * rows, q), down_send, high_recv, {"tile": t - 1})

    def to_high(base, q, n):
        return remote(at(base + rows, q), at(base, q), up_send, low_recv, {"tile": t + 1})

    def spread(base, q, n):
        @pl.when(has_low)
        def _():
            to_low(base, q, n).start()

        @pl.when(has_high)
        def _():
            to_high(base, q, n).start()

    def arrived(base, q, n):
        remote(mine(q), at(base + rows, q), z_send, z_recv.at[n], {"section": s_up}).wait_recv()

    def side(ref, count):
        part = ref.at[pl.ds(0, count)]
        return lambda send, recv, where: remote(part, part, send, recv, where)

    def finish(count):
        @pl.when(has_low)
        def _():
            side(win, count)(up_send, low_recv, {"tile": t - 1}).wait_recv()

        @pl.when(has_high)
        def _():
            side(win, count)(down_send, high_recv, {"tile": t + 1}).wait_recv()

    def finish_sends(count, z_count):
        @pl.when(has_low)
        def _():
            side(win, count)(down_send, high_recv, {"tile": t - 1}).wait_send()

        @pl.when(has_high)
        def _():
            side(win, count)(up_send, low_recv, {"tile": t + 1}).wait_send()

        side(win, z_count)(z_send, low_recv, {"section": s_up}).wait_send()

    @pl.when(s == 0)
    def _():
        for q in range(chunks):
            remote(mine(q), at(rows, q), z_send, z_recv.at[q], {"section": s_up}).start()
            other = (q + half) % chunks
            remote(mine(other), at(rows, other), z_send, z_recv.at[other], {"section": s_down}).start()

        part = WPIECES // (2 * chunks)

        def direct(q, _):
            for src in (0, 2):
                n = src * chunks + q
                arrived(src * 3 * rows, q, n)
                spread(src * 3 * rows, q, n)
                lax.fori_loop((2 * q + src // 2) * part, (2 * q + src // 2 + 1) * part, turn, 0)
            return 0

        lax.fori_loop(0, chunks, direct, 0)

        def relayed(q, _):
            for h in range(2):
                n = chunks + h * half + q
                arrived(3 * rows, h * half + q, n)
                spread(3 * rows, h * half + q, n)
            return 0

        lax.fori_loop(0, half, relayed, 0)
        finish(3 * rows)

    @pl.when((s == 1) | (s == 3))
    def _():
        h = s // 2
        base = (s - 1) * (3 * rows)
        part = WPIECES // (4 * half)
        far = 2
        for q in range(chunks):
            remote(mine(q), at(base + rows, q), z_send, z_recv.at[(s - 1) * chunks + q], {"section": 0}).start()

        def step(q, _):
            own = h * half + q
            held = relay.at[pl.ds(q * CHUNK, CHUNK)]
            arrived(0, own, own)
            remote(at(rows, own), at(rows, own), z_send, z_recv.at[own], {"section": far}).start()
            spread(0, own, own)
            remote(mine(q), held, z_send, relay_recv.at[q], {"section": far}).wait_recv()
            remote(
                held, at(4 * rows, own), z_send, z_recv.at[chunks + own], {"section": 0}
            ).start()
            lax.fori_loop(q * part, (q + 1) * part, turn, 0)
            return 0

        lax.fori_loop(0, half, step, 0)

        def rest(q, _):
            other = (1 - h) * half + q
            arrived(0, other, other)
            spread(0, other, other)
            lax.fori_loop(half * part + q * 3 * part, half * part + (q + 1) * 3 * part, turn, 0)
            return 0

        lax.fori_loop(0, half, rest, 0)
        finish(rows)

    @pl.when(s == 2)
    def _():
        part = WPIECES // half
        for q in range(half):
            held = relay.at[pl.ds(q * CHUNK, CHUNK)]
            remote(mine(q), held, z_send, relay_recv.at[q], {"section": 1}).start()
            remote(mine(half + q), held, z_send, relay_recv.at[q], {"section": 3}).start()

        def step(q, _):
            for n in (q, half + q):
                arrived(0, n, n)
                spread(0, n, n)
            lax.fori_loop(q * part, (q + 1) * part, turn, 0)
            return 0

        lax.fori_loop(0, half, step, 0)
        finish(rows)

    for copy in small_in[1:]:
        copy.wait()
    place_out.wait()

    lane = lax.broadcasted_iota(jnp.int32, (fields, fields), 1)
    sub = lax.broadcasted_iota(jnp.int32, (fields, fields), 0)
    diag = jnp.where(lane == sub, jnp.broadcast_to(kappa[0:1, :], (fields, fields)), 0.0)
    kap = jnp.broadcast_to(jnp.sum(diag, axis=1, keepdims=True), (fields, cells))
    inv = 1.0 / (1.0 + 2.0 * kap + 2.0 * (ZONAL_RATIO * kap))
    a = kap * inv
    b = ZONAL_RATIO * kap * inv

    def forced(r):
        picks, weights = [], []
        for k in range(blocks):
            picks.append(win[index[k, r]])
            weights.append(w[r, k])
        forcing = lax.dot_general(
            jnp.concatenate(picks, axis=1), jnp.concatenate(weights, axis=0), NN, preferred_element_type=F32
        )
        scale = TIME_STEP * mask[pl.ds(r, 1), :].astype(F32)
        return surf[r] + scale * forcing

    def swept(base, low, mid, high):
        zonal = pltpu.roll(mid, 1, 1) + pltpu.roll(mid, cells - 1, 1)
        return base + a * (low + high) + b * zonal

    def advance(state, row):
        levels, bases = state
        levels, bases = [list(x) for x in levels], list(bases)
        bases.append(row * inv)
        levels[0].append(row)
        new = None
        for n in range(SWEEPS):
            if len(levels[n]) < 3:
                return (levels, bases), None
            new = swept(bases[-2 - n], *levels[n][-3:])
            levels[n] = levels[n][-2:]
            if n + 1 < SWEEPS:
                levels[n + 1].append(new)
        return (levels, bases[-SWEEPS - 1:]), new

    low_rows = [forced(r) for r in range(SWEEPS)]
    high_rows = [forced(rows - SWEEPS + r) for r in range(SWEEPS)]
    for r in range(SWEEPS):
        edge[0, r] = low_rows[r]
        edge[1, r] = high_rows[r]
    halo_low = remote(edge.at[0], halo.at[1], halo_send.at[0], halo_recv.at[1], {"tile": t - 1})
    halo_high = remote(edge.at[1], halo.at[0], halo_send.at[1], halo_recv.at[0], {"tile": t + 1})
    pl.when(has_low)(halo_low.start)
    pl.when(has_high)(halo_high.start)

    state = ([[] for _ in range(SWEEPS)], [])
    for r in range(2 * SWEEPS):
        if r < SWEEPS:
            row = low_rows[r]
        else:
            row = forced(r)
            near[0, r - SWEEPS] = row
        state, done = advance(state, row)
        if done is not None:
            out[r - SWEEPS] = done

    def pack(state):
        levels, bases = state
        return tuple(x for level in levels for x in level) + tuple(bases[-SWEEPS:])

    def unpack(flat):
        return [list(flat[2 * n : 2 * n + 2]) for n in range(SWEEPS)], list(flat[2 * SWEEPS :])

    first = 2 * SWEEPS
    count = (rows - 2 * SWEEPS - first) // GROUP - 1

    def put(start, size):
        part = pl.ds(start, size)
        return pltpu.make_async_copy(out.at[part], out_hbm.at[0, part], out_sem)

    def group(g, flat):
        state = unpack(flat)
        for u in range(GROUP):
            r = first + g * GROUP + u
            state, done = advance(state, forced(r))
            out[r - SWEEPS] = done
        put(first - SWEEPS + g * GROUP, GROUP).start()
        return pack(state)

    state = unpack(lax.fori_loop(0, count, group, pack(state)))

    pl.when(has_low)(halo_high.wait_recv)
    pl.when(has_high)(halo_low.wait_recv)

    def end_rows(values, outside, lost):
        values = [jnp.where(lost, 0.0, v) if outside(i) else v for i, v in enumerate(values)]
        bases = [v * inv for v in values]
        level = values
        for n in range(SWEEPS):
            level = [
                jnp.where(lost, 0.0, v) if outside(n + 1 + i) else v
                for i, v in enumerate(
                    swept(bases[n + i], *level[i - 1 : i + 2]) for i in range(1, len(level) - 1)
                )
            ]
        return level

    low_values = [halo[0, r] for r in range(SWEEPS)] + [edge[0, r] for r in range(SWEEPS)]
    low_values += [near[0, r] for r in range(SWEEPS)]
    for r, v in enumerate(end_rows(low_values, lambda i: i < SWEEPS, jnp.logical_not(has_low))):
        out[r] = v
    for r in range(first + count * GROUP, rows):
        if r < rows - SWEEPS:
            row = forced(r)
            if r >= rows - 2 * SWEEPS:
                near[1, r - (rows - 2 * SWEEPS)] = row
        else:
            row = edge[1, r - (rows - SWEEPS)]
        state, done = advance(state, row)
        out[r - SWEEPS] = done

    high_values = [near[1, r] for r in range(SWEEPS)] + [edge[1, r] for r in range(SWEEPS)]
    high_values += [halo[1, r] for r in range(SWEEPS)]
    for r, v in enumerate(end_rows(high_values, lambda i: i >= 2 * SWEEPS, jnp.logical_not(has_high))):
        out[rows - SWEEPS + r] = v

    put(0, SWEEPS).start()
    put(first - SWEEPS + count * GROUP, rows - (first - SWEEPS + count * GROUP)).start()

    pl.when(has_low)(halo_low.wait_send)
    pl.when(has_high)(halo_high.wait_send)

    @pl.when(s == 0)
    def _():
        finish_sends(3 * rows, 2 * rows)

    @pl.when((s == 1) | (s == 3))
    def _():
        finish_sends(rows, 2 * rows)

    @pl.when(s == 2)
    def _():
        finish_sends(rows, rows)

    put(0, rows).wait()

def body(tiles, surface, surface_mask, kappa, remap_weights, remap_columns):
    rows, fields, cells = surface.shape[1:]
    blocks = remap_weights.shape[2]
    chunks = rows // CHUNK
    half = chunks // 2
    block = (rows, fields, cells)
    dma = pltpu.SemaphoreType.DMA
    bf16 = jnp.bfloat16
    return pl.pallas_call(
        functools.partial(kernel, tiles),
        out_shape=jax.ShapeDtypeStruct(surface.shape, F32),
        in_specs=[pl.BlockSpec(memory_space=pltpu.HBM)] * 5,
        out_specs=pl.BlockSpec(memory_space=pl.ANY),
        scratch_shapes=[
            pltpu.VMEM(block, F32),
            pltpu.VMEM((rows, cells), jnp.int32),
            pltpu.VMEM((1, fields), F32),
            pltpu.VMEM((rows, blocks, cells, cells), bf16),
            pltpu.VMEM((blocks, rows), jnp.int32),
            pltpu.VMEM((blocks, rows), jnp.int32),
            pltpu.SMEM((blocks, rows), jnp.int32),
            pltpu.VMEM(block, bf16),
            pltpu.VMEM((9 * rows, fields, cells), bf16),
            pltpu.VMEM((rows // 2, fields, cells), bf16),
            pltpu.VMEM((2, SWEEPS, fields, cells), F32),
            pltpu.VMEM((2, SWEEPS, fields, cells), F32),
            pltpu.VMEM((2, SWEEPS, fields, cells), F32),
            pltpu.VMEM(block, F32),
            dma((4,)),
            dma((WPIECES,)),
            dma((4,)),
            dma(()),
            dma(()),
            dma((3 * chunks,)),
            dma(()),
            dma(()),
            dma(()),
            dma(()),
            dma((half,)),
            dma((2,)),
            dma((2,)),
        ],
        compiler_params=pltpu.CompilerParams(
            collective_id=0, has_side_effects=True, vmem_limit_bytes=60 * 1024 * 1024
        ),
        name="remap_and_sweep",
    )(surface, surface_mask, kappa, remap_weights, remap_columns[0].T)


def solution(mesh):
    return jax.shard_map(
        functools.partial(body, mesh.shape["tile"]),
        mesh=mesh,
        in_specs=(
            P("section", "tile", None, None),
            P("section", "tile", None),
            P("section", None),
            P("section", "tile", None, None, None),
            P("section", "tile", None),
        ),
        out_specs=P("section", "tile", None, None),
        check_vma=False,
    )
```

```python
import functools

import jax
import jax.numpy as jnp
from jax import lax
from jax.experimental import pallas as pl
from jax.experimental.pallas import tpu as pltpu
from jax.sharding import PartitionSpec as P

SWEEPS = 4
TIME_STEP = 0.5
ZONAL_RATIO = 0.25

CHUNK = 16
GROUP = 28
WPIECES = 32

NN = (((1,), (0,)), ((), ()))
F32 = jnp.float32


def remote(src, dst, send_sem, recv_sem, where):
    return pltpu.make_async_remote_copy(
        src_ref=src, dst_ref=dst, send_sem=send_sem, recv_sem=recv_sem,
        device_id=where, device_id_type=pl.DeviceIdType.MESH,
    )


def kernel(
    tiles, surf_hbm, mask_hbm, kappa_hbm, w_hbm, cols_hbm, out_hbm,
    surf, mask, kappa, w, cols, place, index, sent, win, relay, edge, near, halo, out,
    surf_sem, w_sem, in_sem, out_sem,
    z_send, z_recv, up_send, down_send, low_recv, high_recv, relay_recv, halo_send, halo_recv,
):
    rows, fields, cells = surf.shape
    blocks = w.shape[1]
    chunks = rows // CHUNK
    half = chunks // 2
    total = rows * tiles
    s = lax.axis_index("section")
    t = lax.axis_index("tile")
    s_up, s_down = lax.rem(s + 1, 4), lax.rem(s + 3, 4)
    has_low, has_high = t > 0, t < tiles - 1

    barrier = pltpu.get_barrier_semaphore()
    for where in ({"section": s_up}, {"section": s_down}):
        pl.semaphore_signal(barrier, inc=1, device_id=where, device_id_type=pl.DeviceIdType.MESH)

    @pl.when(has_low)
    def _():
        pl.semaphore_signal(barrier, inc=1, device_id={"tile": t - 1}, device_id_type=pl.DeviceIdType.MESH)

    @pl.when(has_high)
    def _():
        pl.semaphore_signal(barrier, inc=1, device_id={"tile": t + 1}, device_id_type=pl.DeviceIdType.MESH)

    surf_in = [
        pltpu.make_async_copy(
            surf_hbm.at[0, pl.ds(p * (rows // 4), rows // 4)], surf.at[pl.ds(p * (rows // 4), rows // 4)], surf_sem.at[p]
        )
        for p in range(4)
    ]
    for copy in surf_in:
        copy.start()
    small_in = [
        pltpu.make_async_copy(cols_hbm, cols, in_sem.at[0]),
        pltpu.make_async_copy(mask_hbm.at[0], mask, in_sem.at[1]),
        pltpu.make_async_copy(kappa_hbm, kappa, in_sem.at[2]),
    ]
    for copy in small_in:
        copy.start()
    piece = rows // WPIECES

    def w_in(p):
        part = pl.ds(p * piece, piece)
        return pltpu.make_async_copy(w_hbm.at[0, part], w.at[part], w_sem.at[p])

    def turn(p, _):
        w_in(p).wait()
        for r in range(piece):
            for k in range(blocks):
                w[p * piece + r, k] = w[p * piece + r, k].T
        return 0

    for p in range(4):
        surf_in[p].wait()
        part = pl.ds(p * (rows // 4), rows // 4)
        sent[part] = surf[part].astype(jnp.bfloat16)
    for p in range(WPIECES):
        w_in(p).start()

    small_in[0].wait()
    offset = (1 - t) * rows - jnp.where(s == 0, 3 * rows, 0)
    column = cols[...]
    place[...] = jnp.clip(column - (column // total) * (total - 3 * rows) + offset, 0, 9 * rows - 1)
    place_out = pltpu.make_async_copy(place, index, in_sem.at[3])
    place_out.start()

    pl.semaphore_wait(barrier, 2 + has_low.astype(jnp.int32) + has_high.astype(jnp.int32))

    def at(start, q):
        return win.at[pl.ds(start + q * CHUNK, CHUNK)]

    def mine(q):
        return sent.at[pl.ds(q * CHUNK, CHUNK)]

    def to_low(base, q, n):
        return remote(at(base + rows, q), at(base + 2 * rows, q), down_send, high_recv, {"tile": t - 1})

    def to_high(base, q, n):
        return remote(at(base + rows, q), at(base, q), up_send, low_recv, {"tile": t + 1})

    def spread(base, q, n):
        @pl.when(has_low)
        def _():
            to_low(base, q, n).start()

        @pl.when(has_high)
        def _():
            to_high(base, q, n).start()

    def arrived(base, q, n):
        remote(mine(q), at(base + rows, q), z_send, z_recv.at[n], {"section": s_up}).wait_recv()

    def side(ref, count):
        part = ref.at[pl.ds(0, count)]
        return lambda send, recv, where: remote(part, part, send, recv, where)

    def finish(count):
        @pl.when(has_low)
        def _():
            side(win, count)(up_send, low_recv, {"tile": t - 1}).wait_recv()

        @pl.when(has_high)
        def _():
            side(win, count)(down_send, high_recv, {"tile": t + 1}).wait_recv()

    def finish_sends(count, z_count):
        @pl.when(has_low)
        def _():
            side(win, count)(down_send, high_recv, {"tile": t - 1}).wait_send()

        @pl.when(has_high)
        def _():
            side(win, count)(up_send, low_recv, {"tile": t + 1}).wait_send()

        side(win, z_count)(z_send, low_recv, {"section": s_up}).wait_send()

    @pl.when(s == 0)
    def _():
        for q in range(chunks):
            remote(mine(q), at(rows, q), z_send, z_recv.at[q], {"section": s_up}).start()
            other = (q + half) % chunks
            remote(mine(other), at(rows, other), z_send, z_recv.at[other], {"section": s_down}).start()

        part = WPIECES // (2 * chunks)

        def direct(q, _):
            for src in (0, 2):
                n = src * chunks + q
                arrived(src * 3 * rows, q, n)
                spread(src * 3 * rows, q, n)
                lax.fori_loop((2 * q + src // 2) * part, (2 * q + src // 2 + 1) * part, turn, 0)
            return 0

        lax.fori_loop(0, chunks, direct, 0)

        def relayed(q, _):
            for h in range(2):
                n = chunks + h * half + q
                arrived(3 * rows, h * half + q, n)
                spread(3 * rows, h * half + q, n)
            return 0

        lax.fori_loop(0, half, relayed, 0)
        finish(3 * rows)

    @pl.when((s == 1) | (s == 3))
    def _():
        h = s // 2
        base = (s - 1) * (3 * rows)
        part = WPIECES // (4 * half)
        far = 2
        for q in range(chunks):
            remote(mine(q), at(base + rows, q), z_send, z_recv.at[(s - 1) * chunks + q], {"section": 0}).start()

        def step(q, _):
            own = h * half + q
            held = relay.at[pl.ds(q * CHUNK, CHUNK)]
            arrived(0, own, own)
            remote(at(rows, own), at(rows, own), z_send, z_recv.at[own], {"section": far}).start()
            spread(0, own, own)
            remote(mine(q), held, z_send, relay_recv.at[q], {"section": far}).wait_recv()
            remote(
                held, at(4 * rows, own), z_send, z_recv.at[chunks + own], {"section": 0}
            ).start()
            lax.fori_loop(q * part, (q + 1) * part, turn, 0)
            return 0

        lax.fori_loop(0, half, step, 0)

        def rest(q, _):
            other = (1 - h) * half + q
            arrived(0, other, other)
            spread(0, other, other)
            lax.fori_loop(half * part + q * 3 * part, half * part + (q + 1) * 3 * part, turn, 0)
            return 0

        lax.fori_loop(0, half, rest, 0)
        finish(rows)

    @pl.when(s == 2)
    def _():
        part = WPIECES // half
        for q in range(half):
            held = relay.at[pl.ds(q * CHUNK, CHUNK)]
            remote(mine(q), held, z_send, relay_recv.at[q], {"section": 1}).start()
            remote(mine(half + q), held, z_send, relay_recv.at[q], {"section": 3}).start()

        def step(q, _):
            for n in (q, half + q):
                arrived(0, n, n)
                spread(0, n, n)
            lax.fori_loop(q * part, (q + 1) * part, turn, 0)
            return 0

        lax.fori_loop(0, half, step, 0)
        finish(rows)

    for copy in small_in[1:]:
        copy.wait()
    place_out.wait()

    lane = lax.broadcasted_iota(jnp.int32, (fields, fields), 1)
    sub = lax.broadcasted_iota(jnp.int32, (fields, fields), 0)
    diag = jnp.where(lane == sub, jnp.broadcast_to(kappa[0:1, :], (fields, fields)), 0.0)
    kap = jnp.broadcast_to(jnp.sum(diag, axis=1, keepdims=True), (fields, cells))
    inv = 1.0 / (1.0 + 2.0 * kap + 2.0 * (ZONAL_RATIO * kap))
    a = kap * inv
    b = ZONAL_RATIO * kap * inv

    def forced(r):
        picks, weights = [], []
        for k in range(blocks):
            picks.append(win[index[k, r]])
            weights.append(w[r, k])
        forcing = lax.dot_general(
            jnp.concatenate(picks, axis=1), jnp.concatenate(weights, axis=0), NN, preferred_element_type=F32
        )
        scale = TIME_STEP * mask[pl.ds(r, 1), :].astype(F32)
        return surf[r] + scale * forcing

    def swept(base, low, mid, high):
        zonal = pltpu.roll(mid, 1, 1) + pltpu.roll(mid, cells - 1, 1)
        return base + a * (low + high) + b * zonal

    def advance(state, row):
        levels, bases = state
        levels, bases = [list(x) for x in levels], list(bases)
        bases.append(row * inv)
        levels[0].append(row)
        new = None
        for n in range(SWEEPS):
            if len(levels[n]) < 3:
                return (levels, bases), None
            new = swept(bases[-2 - n], *levels[n][-3:])
            levels[n] = levels[n][-2:]
            if n + 1 < SWEEPS:
                levels[n + 1].append(new)
        return (levels, bases[-SWEEPS - 1:]), new

    low_rows = [forced(r) for r in range(SWEEPS)]
    high_rows = [forced(rows - SWEEPS + r) for r in range(SWEEPS)]
    for r in range(SWEEPS):
        edge[0, r] = low_rows[r]
        edge[1, r] = high_rows[r]
    halo_low = remote(edge.at[0], halo.at[1], halo_send.at[0], halo_recv.at[1], {"tile": t - 1})
    halo_high = remote(edge.at[1], halo.at[0], halo_send.at[1], halo_recv.at[0], {"tile": t + 1})
    pl.when(has_low)(halo_low.start)
    pl.when(has_high)(halo_high.start)

    state = ([[] for _ in range(SWEEPS)], [])
    for r in range(2 * SWEEPS):
        if r < SWEEPS:
            row = low_rows[r]
        else:
            row = forced(r)
            near[0, r - SWEEPS] = row
        state, done = advance(state, row)
        if done is not None:
            out[r - SWEEPS] = done

    def pack(state):
        levels, bases = state
        return tuple(x for level in levels for x in level) + tuple(bases[-SWEEPS:])

    def unpack(flat):
        return [list(flat[2 * n : 2 * n + 2]) for n in range(SWEEPS)], list(flat[2 * SWEEPS :])

    first = 2 * SWEEPS
    count = (rows - 2 * SWEEPS - first) // GROUP - 1

    def put(start, size):
        part = pl.ds(start, size)
        return pltpu.make_async_copy(out.at[part], out_hbm.at[0, part], out_sem)

    def group(g, flat):
        state = unpack(flat)
        for u in range(GROUP):
            r = first + g * GROUP + u
            state, done = advance(state, forced(r))
            out[r - SWEEPS] = done
        put(first - SWEEPS + g * GROUP, GROUP).start()
        return pack(state)

    state = unpack(lax.fori_loop(0, count, group, pack(state)))

    pl.when(has_low)(halo_high.wait_recv)
    pl.when(has_high)(halo_low.wait_recv)

    def end_rows(values, outside, lost):
        values = [jnp.where(lost, 0.0, v) if outside(i) else v for i, v in enumerate(values)]
        bases = [v * inv for v in values]
        level = values
        for n in range(SWEEPS):
            level = [
                jnp.where(lost, 0.0, v) if outside(n + 1 + i) else v
                for i, v in enumerate(
                    swept(bases[n + i], *level[i - 1 : i + 2]) for i in range(1, len(level) - 1)
                )
            ]
        return level

    low_values = [halo[0, r] for r in range(SWEEPS)] + [edge[0, r] for r in range(SWEEPS)]
    low_values += [near[0, r] for r in range(SWEEPS)]
    for r, v in enumerate(end_rows(low_values, lambda i: i < SWEEPS, jnp.logical_not(has_low))):
        out[r] = v
    for r in range(first + count * GROUP, rows):
        if r < rows - SWEEPS:
            row = forced(r)
            if r >= rows - 2 * SWEEPS:
                near[1, r - (rows - 2 * SWEEPS)] = row
        else:
            row = edge[1, r - (rows - SWEEPS)]
        state, done = advance(state, row)
        out[r - SWEEPS] = done

    high_values = [near[1, r] for r in range(SWEEPS)] + [edge[1, r] for r in range(SWEEPS)]
    high_values += [halo[1, r] for r in range(SWEEPS)]
    for r, v in enumerate(end_rows(high_values, lambda i: i >= 2 * SWEEPS, jnp.logical_not(has_high))):
        out[rows - SWEEPS + r] = v

    put(0, SWEEPS).start()
    put(first - SWEEPS + count * GROUP, rows - (first - SWEEPS + count * GROUP)).start()

    pl.when(has_low)(halo_low.wait_send)
    pl.when(has_high)(halo_high.wait_send)

    @pl.when(s == 0)
    def _():
        finish_sends(3 * rows, 2 * rows)

    @pl.when((s == 1) | (s == 3))
    def _():
        finish_sends(rows, 2 * rows)

    @pl.when(s == 2)
    def _():
        finish_sends(rows, rows)

    put(0, rows).wait()

def body(tiles, surface, surface_mask, kappa, remap_weights, remap_columns):
    rows, fields, cells = surface.shape[1:]
    blocks = remap_weights.shape[2]
    chunks = rows // CHUNK
    half = chunks // 2
    block = (rows, fields, cells)
    dma = pltpu.SemaphoreType.DMA
    bf16 = jnp.bfloat16
    return pl.pallas_call(
        functools.partial(kernel, tiles),
        out_shape=jax.ShapeDtypeStruct(surface.shape, F32),
        in_specs=[pl.BlockSpec(memory_space=pltpu.HBM)] * 5,
        out_specs=pl.BlockSpec(memory_space=pl.ANY),
        scratch_shapes=[
            pltpu.VMEM(block, F32),
            pltpu.VMEM((rows, cells), jnp.int32),
            pltpu.VMEM((1, fields), F32),
            pltpu.VMEM((rows, blocks, cells, cells), bf16),
            pltpu.VMEM((blocks, rows), jnp.int32),
            pltpu.VMEM((blocks, rows), jnp.int32),
            pltpu.SMEM((blocks, rows), jnp.int32),
            pltpu.VMEM(block, bf16),
            pltpu.VMEM((9 * rows, fields, cells), bf16),
            pltpu.VMEM((rows // 2, fields, cells), bf16),
            pltpu.VMEM((2, SWEEPS, fields, cells), F32),
            pltpu.VMEM((2, SWEEPS, fields, cells), F32),
            pltpu.VMEM((2, SWEEPS, fields, cells), F32),
            pltpu.VMEM(block, F32),
            dma((4,)),
            dma((WPIECES,)),
            dma((4,)),
            dma(()),
            dma(()),
            dma((3 * chunks,)),
            dma(()),
            dma(()),
            dma(()),
            dma(()),
            dma((half,)),
            dma((2,)),
            dma((2,)),
        ],
        compiler_params=pltpu.CompilerParams(
            collective_id=0, has_side_effects=True, vmem_limit_bytes=44 * 1024 * 1024
        ),
        name="remap_and_sweep",
    )(*[pltpu.with_memory_space_constraint(v, pltpu.HBM) for v in (surface, surface_mask, kappa, remap_weights, remap_columns[0].T)])


def solution(mesh):
    return jax.shard_map(
        functools.partial(body, mesh.shape["tile"]),
        mesh=mesh,
        in_specs=(
            P("section", "tile", None, None),
            P("section", "tile", None),
            P("section", None),
            P("section", "tile", None, None, None),
            P("section", "tile", None),
        ),
        out_specs=P("section", "tile", None, None),
        check_vma=False,
    )
```

```python
import functools

import jax
import jax.numpy as jnp
from jax import lax
from jax.experimental import pallas as pl
from jax.experimental.pallas import tpu as pltpu
from jax.sharding import PartitionSpec as P

SWEEPS = 4
TIME_STEP = 0.5
ZONAL_RATIO = 0.25

CHUNK = 16
TAIL = 8
WPIECES = 32

NN = (((1,), (0,)), ((), ()))
F32 = jnp.float32


def remote(src, dst, send_sem, recv_sem, where):
    return pltpu.make_async_remote_copy(
        src_ref=src, dst_ref=dst, send_sem=send_sem, recv_sem=recv_sem,
        device_id=where, device_id_type=pl.DeviceIdType.MESH,
    )


def kernel(
    tiles, surf_hbm, mask_hbm, kappa_hbm, w_hbm, cols_hbm, out_hbm,
    surf, mask, kappa, w, cols, place, index, sent, win, relay, edge, near, halo, out,
    surf_sem, w_sem, in_sem, out_sem,
    z_send, z_recv, up_send, down_send, low_recv, high_recv, relay_recv, halo_send, halo_recv,
):
    rows, fields, cells = surf.shape
    blocks = w.shape[1]
    chunks = rows // CHUNK
    half = chunks // 2
    total = rows * tiles
    s = lax.axis_index("section")
    t = lax.axis_index("tile")
    s_up, s_down = lax.rem(s + 1, 4), lax.rem(s + 3, 4)
    has_low, has_high = t > 0, t < tiles - 1

    barrier = pltpu.get_barrier_semaphore()
    for where in ({"section": s_up}, {"section": s_down}):
        pl.semaphore_signal(barrier, inc=1, device_id=where, device_id_type=pl.DeviceIdType.MESH)

    @pl.when(has_low)
    def _():
        pl.semaphore_signal(barrier, inc=1, device_id={"tile": t - 1}, device_id_type=pl.DeviceIdType.MESH)

    @pl.when(has_high)
    def _():
        pl.semaphore_signal(barrier, inc=1, device_id={"tile": t + 1}, device_id_type=pl.DeviceIdType.MESH)

    surf_in = [
        pltpu.make_async_copy(
            surf_hbm.at[0, pl.ds(p * (rows // 4), rows // 4)], surf.at[pl.ds(p * (rows // 4), rows // 4)], surf_sem.at[p]
        )
        for p in range(4)
    ]
    for copy in surf_in:
        copy.start()
    small_in = [
        pltpu.make_async_copy(cols_hbm, cols, in_sem.at[0]),
        pltpu.make_async_copy(mask_hbm.at[0], mask, in_sem.at[1]),
        pltpu.make_async_copy(kappa_hbm, kappa, in_sem.at[2]),
    ]
    for copy in small_in:
        copy.start()
    piece = rows // WPIECES

    def w_in(p):
        part = pl.ds(p * piece, piece)
        return pltpu.make_async_copy(w_hbm.at[0, part], w.at[part], w_sem.at[p])

    def turn(p, _):
        w_in(p).wait()
        for r in range(piece):
            for k in range(blocks):
                w[p * piece + r, k] = w[p * piece + r, k].T
        return 0

    for p in range(4):
        surf_in[p].wait()
        part = pl.ds(p * (rows // 4), rows // 4)
        sent[part] = surf[part].astype(jnp.bfloat16)
    for p in range(WPIECES):
        w_in(p).start()

    small_in[0].wait()
    offset = (1 - t) * rows - jnp.where(s == 0, 3 * rows, 0)
    column = cols[...]
    place[...] = jnp.clip(column - (column // total) * (total - 3 * rows) + offset, 0, 9 * rows - 1)
    place_out = pltpu.make_async_copy(place, index, in_sem.at[3])
    place_out.start()

    pl.semaphore_wait(barrier, 2 + has_low.astype(jnp.int32) + has_high.astype(jnp.int32))

    def at(start, q):
        return win.at[pl.ds(start + q * CHUNK, CHUNK)]

    def mine(q):
        return sent.at[pl.ds(q * CHUNK, CHUNK)]

    def to_low(base, q, n):
        return remote(at(base + rows, q), at(base + 2 * rows, q), down_send, high_recv, {"tile": t - 1})

    def to_high(base, q, n):
        return remote(at(base + rows, q), at(base, q), up_send, low_recv, {"tile": t + 1})

    def spread(base, q, n):
        @pl.when(has_low)
        def _():
            to_low(base, q, n).start()

        @pl.when(has_high)
        def _():
            to_high(base, q, n).start()

    def arrived(base, q, n):
        remote(mine(q), at(base + rows, q), z_send, z_recv.at[n], {"section": s_up}).wait_recv()

    def side(ref, count):
        part = ref.at[pl.ds(0, count)]
        return lambda send, recv, where: remote(part, part, send, recv, where)

    def finish(count):
        @pl.when(has_low)
        def _():
            side(win, count)(up_send, low_recv, {"tile": t - 1}).wait_recv()

        @pl.when(has_high)
        def _():
            side(win, count)(down_send, high_recv, {"tile": t + 1}).wait_recv()

    def finish_sends(count, z_count):
        @pl.when(has_low)
        def _():
            side(win, count)(down_send, high_recv, {"tile": t - 1}).wait_send()

        @pl.when(has_high)
        def _():
            side(win, count)(up_send, low_recv, {"tile": t + 1}).wait_send()

        side(win, z_count)(z_send, low_recv, {"section": s_up}).wait_send()

    @pl.when(s == 0)
    def _():
        for q in range(chunks):
            remote(mine(q), at(rows, q), z_send, z_recv.at[q], {"section": s_up}).start()
            other = (q + half) % chunks
            remote(mine(other), at(rows, other), z_send, z_recv.at[other], {"section": s_down}).start()

        part = WPIECES // (2 * chunks)

        def direct(q, _):
            for src in (0, 2):
                n = src * chunks + q
                arrived(src * 3 * rows, q, n)
                spread(src * 3 * rows, q, n)
                lax.fori_loop((2 * q + src // 2) * part, (2 * q + src // 2 + 1) * part, turn, 0)
            return 0

        lax.fori_loop(0, chunks, direct, 0)

        def relayed(q, _):
            for h in range(2):
                n = chunks + h * half + q
                arrived(3 * rows, h * half + q, n)
                spread(3 * rows, h * half + q, n)
            return 0

        lax.fori_loop(0, half, relayed, 0)
        finish(3 * rows)

    @pl.when((s == 1) | (s == 3))
    def _():
        h = s // 2
        base = (s - 1) * (3 * rows)
        part = WPIECES // (4 * half)
        far = 2
        for q in range(chunks):
            remote(mine(q), at(base + rows, q), z_send, z_recv.at[(s - 1) * chunks + q], {"section": 0}).start()

        def step(q, _):
            own = h * half + q
            held = relay.at[pl.ds(q * CHUNK, CHUNK)]
            arrived(0, own, own)
            remote(at(rows, own), at(rows, own), z_send, z_recv.at[own], {"section": far}).start()
            spread(0, own, own)
            remote(mine(q), held, z_send, relay_recv.at[q], {"section": far}).wait_recv()
            remote(
                held, at(4 * rows, own), z_send, z_recv.at[chunks + own], {"section": 0}
            ).start()
            lax.fori_loop(q * part, (q + 1) * part, turn, 0)
            return 0

        lax.fori_loop(0, half, step, 0)

        def rest(q, _):
            other = (1 - h) * half + q
            arrived(0, other, other)
            spread(0, other, other)
            lax.fori_loop(half * part + q * 3 * part, half * part + (q + 1) * 3 * part, turn, 0)
            return 0

        lax.fori_loop(0, half, rest, 0)
        finish(rows)

    @pl.when(s == 2)
    def _():
        part = WPIECES // half
        for q in range(half):
            held = relay.at[pl.ds(q * CHUNK, CHUNK)]
            remote(mine(q), held, z_send, relay_recv.at[q], {"section": 1}).start()
            remote(mine(half + q), held, z_send, relay_recv.at[q], {"section": 3}).start()

        def step(q, _):
            for n in (q, half + q):
                arrived(0, n, n)
                spread(0, n, n)
            lax.fori_loop(q * part, (q + 1) * part, turn, 0)
            return 0

        lax.fori_loop(0, half, step, 0)
        finish(rows)

    for copy in small_in[1:]:
        copy.wait()
    place_out.wait()

    lane = lax.broadcasted_iota(jnp.int32, (fields, fields), 1)
    sub = lax.broadcasted_iota(jnp.int32, (fields, fields), 0)
    diag = jnp.where(lane == sub, jnp.broadcast_to(kappa[0:1, :], (fields, fields)), 0.0)
    kap = jnp.broadcast_to(jnp.sum(diag, axis=1, keepdims=True), (fields, cells))
    inv = 1.0 / (1.0 + 2.0 * kap + 2.0 * (ZONAL_RATIO * kap))
    a = kap * inv
    b = ZONAL_RATIO * kap * inv

    def forced(r):
        picks, weights = [], []
        for k in range(blocks):
            picks.append(win[index[k, r]])
            weights.append(w[r, k])
        forcing = lax.dot_general(
            jnp.concatenate(picks, axis=1), jnp.concatenate(weights, axis=0), NN, preferred_element_type=F32
        )
        scale = TIME_STEP * mask[pl.ds(r, 1), :].astype(F32)
        return surf[r] + scale * forcing

    def swept(base, low, mid, high):
        zonal = pltpu.roll(mid, 1, 1) + pltpu.roll(mid, cells - 1, 1)
        return base + a * (low + high) + b * zonal

    def advance(state, row):
        levels, bases = state
        levels, bases = [list(x) for x in levels], list(bases)
        bases.append(row * inv)
        levels[0].append(row)
        new = None
        for n in range(SWEEPS):
            if len(levels[n]) < 3:
                return (levels, bases), None
            new = swept(bases[-2 - n], *levels[n][-3:])
            levels[n] = levels[n][-2:]
            if n + 1 < SWEEPS:
                levels[n + 1].append(new)
        return (levels, bases[-SWEEPS - 1:]), new

    low_rows = [forced(r) for r in range(SWEEPS)]
    high_rows = [forced(rows - SWEEPS + r) for r in range(SWEEPS)]
    for r in range(SWEEPS):
        edge[0, r] = low_rows[r]
        edge[1, r] = high_rows[r]
    halo_low = remote(edge.at[0], halo.at[1], halo_send.at[0], halo_recv.at[1], {"tile": t - 1})
    halo_high = remote(edge.at[1], halo.at[0], halo_send.at[1], halo_recv.at[0], {"tile": t + 1})
    pl.when(has_low)(halo_low.start)
    pl.when(has_high)(halo_high.start)

    state = ([[] for _ in range(SWEEPS)], [])
    for r in range(2 * SWEEPS):
        if r < SWEEPS:
            row = low_rows[r]
        else:
            row = forced(r)
            near[0, r - SWEEPS] = row
        state, done = advance(state, row)
        if done is not None:
            out[r - SWEEPS] = done

    def put(start, size):
        part = pl.ds(start, size)
        return pltpu.make_async_copy(out.at[part], out_hbm.at[0, part], out_sem)

    def interior(state, first, last):
        for r in range(first, last):
            if r < rows - SWEEPS:
                row = forced(r)
                if r >= rows - 2 * SWEEPS:
                    near[1, r - (rows - 2 * SWEEPS)] = row
            else:
                row = edge[1, r - (rows - SWEEPS)]
            state, done = advance(state, row)
            if done is not None:
                out[r - SWEEPS] = done
        return state

    state = interior(state, 2 * SWEEPS, rows - TAIL)
    put(SWEEPS, rows - TAIL - 2 * SWEEPS).start()

    pl.when(has_low)(halo_high.wait_recv)
    pl.when(has_high)(halo_low.wait_recv)

    def end_rows(values, outside, lost):
        values = [jnp.where(lost, 0.0, v) if outside(i) else v for i, v in enumerate(values)]
        bases = [v * inv for v in values]
        level = values
        for n in range(SWEEPS):
            level = [
                jnp.where(lost, 0.0, v) if outside(n + 1 + i) else v
                for i, v in enumerate(
                    swept(bases[n + i], *level[i - 1 : i + 2]) for i in range(1, len(level) - 1)
                )
            ]
        return level

    low_values = [halo[0, r] for r in range(SWEEPS)] + [edge[0, r] for r in range(SWEEPS)]
    low_values += [near[0, r] for r in range(SWEEPS)]
    for r, v in enumerate(end_rows(low_values, lambda i: i < SWEEPS, jnp.logical_not(has_low))):
        out[r] = v
    interior(state, rows - TAIL, rows)
    high_values = [near[1, r] for r in range(SWEEPS)] + [edge[1, r] for r in range(SWEEPS)]
    high_values += [halo[1, r] for r in range(SWEEPS)]
    for r, v in enumerate(end_rows(high_values, lambda i: i >= 2 * SWEEPS, jnp.logical_not(has_high))):
        out[rows - SWEEPS + r] = v

    put(0, SWEEPS).start()
    put(rows - TAIL - SWEEPS, TAIL + SWEEPS).start()

    pl.when(has_low)(halo_low.wait_send)
    pl.when(has_high)(halo_high.wait_send)

    @pl.when(s == 0)
    def _():
        finish_sends(3 * rows, 2 * rows)

    @pl.when((s == 1) | (s == 3))
    def _():
        finish_sends(rows, 2 * rows)

    @pl.when(s == 2)
    def _():
        finish_sends(rows, rows)

    put(0, rows).wait()

def body(tiles, surface, surface_mask, kappa, remap_weights, remap_columns):
    rows, fields, cells = surface.shape[1:]
    blocks = remap_weights.shape[2]
    chunks = rows // CHUNK
    half = chunks // 2
    block = (rows, fields, cells)
    dma = pltpu.SemaphoreType.DMA
    bf16 = jnp.bfloat16
    return pl.pallas_call(
        functools.partial(kernel, tiles),
        out_shape=jax.ShapeDtypeStruct(surface.shape, F32),
        in_specs=[pl.BlockSpec(memory_space=pltpu.HBM)] * 5,
        out_specs=pl.BlockSpec(memory_space=pl.ANY),
        scratch_shapes=[
            pltpu.VMEM(block, F32),
            pltpu.VMEM((rows, cells), jnp.int32),
            pltpu.VMEM((1, fields), F32),
            pltpu.VMEM((rows, blocks, cells, cells), bf16),
            pltpu.VMEM((blocks, rows), jnp.int32),
            pltpu.VMEM((blocks, rows), jnp.int32),
            pltpu.SMEM((blocks, rows), jnp.int32),
            pltpu.VMEM(block, bf16),
            pltpu.VMEM((9 * rows, fields, cells), bf16),
            pltpu.VMEM((rows // 2, fields, cells), bf16),
            pltpu.VMEM((2, SWEEPS, fields, cells), F32),
            pltpu.VMEM((2, SWEEPS, fields, cells), F32),
            pltpu.VMEM((2, SWEEPS, fields, cells), F32),
            pltpu.VMEM(block, F32),
            dma((4,)),
            dma((WPIECES,)),
            dma((4,)),
            dma(()),
            dma(()),
            dma((3 * chunks,)),
            dma(()),
            dma(()),
            dma(()),
            dma(()),
            dma((half,)),
            dma((2,)),
            dma((2,)),
        ],
        compiler_params=pltpu.CompilerParams(
            collective_id=0, has_side_effects=True, vmem_limit_bytes=44 * 1024 * 1024
        ),
        name="remap_and_sweep",
    )(*[pltpu.with_memory_space_constraint(v, pltpu.HBM) for v in (surface, surface_mask, kappa, remap_weights, remap_columns[0].T)])


def solution(mesh):
    return jax.shard_map(
        functools.partial(body, mesh.shape["tile"]),
        mesh=mesh,
        in_specs=(
            P("section", "tile", None, None),
            P("section", "tile", None),
            P("section", None),
            P("section", "tile", None, None, None),
            P("section", "tile", None),
        ),
        out_specs=P("section", "tile", None, None),
        check_vma=False,
    )
```
